256 devices in a mesh: blk: 32 (over y_hi, z, core), lag: 8 (over y_lo, x).
Axes of the slice: x: 4, y: 4 (y_hi: 2, y_lo: 2; y = y_hi * 2 + y_lo), z: 8, core: 2. Of those that a mesh axis runs over, the one named last changes fastest.
Arguments:
- spectra: bfloat16 [4096, 3, 2, 1024], P('blk', None, None, 'lag'), may hold values from -6 to 6
- band: int32 [4096, 2], P('blk'), may hold values from 0 to 1024, as said below
- pair_lists: int32 [32, 17, 96, 2], P('blk'), may hold values from 0 to 127
- pair_counts: int32 [32, 17], P('blk'), may hold values from 32 to 96, as said below
Outputs:
- gradient: float32 [4096, 3, 2, 1024], P('blk', None, None, 'lag')
The draws below stay inside these ranges and needn't reach their ends.
Inputs may be any that keep to these rules, and one draw needn't show every extreme that they name: band[s, 0] < band[s, 1]; band[s, 0] is at most 128 and band[s, 1] at least 896; some station starts at 0 and some ends at 1024. `pair_counts`: at least a third of the slots are used; in every block one offset uses all 96 slots.
All inputs are finite; a program needn't handle non-finite values.
Results may differ from the reference program's by a relative error of at most 0.0045.
Values may be sent and summed in bfloat16 or wider, within the bound.
No kernel may reach another device: no remote copies, remote signals or barrier semaphores. Data moves between devices by JAX's collectives and lax.ppermute only.
A program may use at most 64 MiB of HBM per device.

```python
import jax
import jax.numpy as jnp
from jax import lax

STA_DEV = 128
P_MAX = 96
F = 1024
LAGS = 2048
BLOCKS = 32
STEPS = 17
STATIONS = 4096


def draw_spectra(key, part):
    base = jax.random.fold_in(key, 37)
    key_noise, key_common, key_sign = jax.random.split(base, 3)
    shape = (STATIONS, 3, 2, F)
    signs = (jax.random.randint(key_sign, (STATIONS, 1, 1, 1), 0, 2) * 2 - 1).astype(jnp.float32)
    noise = jax.random.normal(key_noise, shape, jnp.float32)
    common = jnp.clip(jax.random.normal(key_common, (1, 3, 2, F), jnp.float32), -2.5, 2.5)
    amplitude = jnp.ones((F,), jnp.float32)
    values = noise + signs * amplitude[None, None, None, :] * common
    return jnp.clip(values, -6.0, 6.0).astype(jnp.bfloat16)


def draw_band(key, part):
    key_lo, key_hi, key_first, key_last = jax.random.split(jax.random.fold_in(key, 11), 4)
    lower = jax.random.randint(key_lo, (STATIONS,), 0, F // 8 + 1)
    upper = jax.random.randint(key_hi, (STATIONS,), F - F // 8, F + 1)
    station_ids = jnp.arange(STATIONS, dtype=jnp.int32)
    first_pick = jax.random.randint(key_first, (), 0, STATIONS)
    last_pick = jax.random.randint(key_last, (), 0, STATIONS)
    lower = jnp.where(station_ids == first_pick, 0, lower)
    upper = jnp.where(station_ids == last_pick, F, upper)
    return jnp.stack([lower, upper], 1).astype(jnp.int32)


def draw_pair_counts(key, part):
    key_base, key_full = jax.random.split(jax.random.fold_in(key, 23))
    base = jax.random.randint(key_base, (BLOCKS, STEPS), P_MAX // 3, P_MAX + 1)
    full_step = jax.random.randint(key_full, (BLOCKS, 1), 0, STEPS)
    step_ids = jnp.arange(STEPS, dtype=jnp.int32)[None, :]
    return jnp.where(step_ids == full_step, P_MAX, base).astype(jnp.int32)


def with_ends(entries, rng, smallest, top_value):
    longest = entries.shape.index(max(entries.shape))
    spots = []
    for shift in (0, 1):
        where = [jax.random.randint(jax.random.fold_in(rng, axis), (), 0, length) for axis, length in enumerate(entries.shape)]
        where[longest] = (where[longest] + shift) % entries.shape[longest]
        spots.append(tuple(where))
    return entries.at[spots[0]].set(smallest).at[spots[1]].set(top_value)


def setup_inputs(seed: int = 0) -> dict:
    keys = jax.random.split(jax.random.key(seed), 5)
    return {
        "spectra": draw_spectra(jax.random.fold_in(keys[4], 71), 0),
        "band": draw_band(jax.random.fold_in(keys[4], 71), 0),
        "pair_lists": with_ends(jax.random.randint(keys[2], (BLOCKS, STEPS, P_MAX, 2), 0, STA_DEV), jax.random.fold_in(keys[2], 1), 0, STA_DEV - 1).astype(jnp.int32),
        "pair_counts": draw_pair_counts(jax.random.fold_in(keys[4], 71), 0),
    }


def phase_table(freq_ids, lag_ids, lag_total, freq_total):
    turns = freq_ids[:, None] * lag_ids[None, :] % lag_total
    angle = turns.astype(jnp.float32) * (2.0 * jnp.pi / lag_total)
    factor = 1.0 / jnp.sqrt(jnp.float32(freq_total))
    return jnp.stack([jnp.cos(angle) * factor, -jnp.sin(angle) * factor], 0).astype(jnp.bfloat16)

def whiten(spectra, band, freq_ids):
    values = spectra.astype(jnp.float32)
    meansq = lax.optimization_barrier(jnp.mean(values * values, axis=(1, 2)))
    inside = (freq_ids[None, :] >= band[:, 0:1]) & (freq_ids[None, :] < band[:, 1:2])
    factor = jnp.where(inside, 1.0 / jnp.sqrt(jnp.maximum(meansq, 0.25)), 0.0)
    return (values * factor[:, None, None, :]).astype(jnp.bfloat16)

def reference(spectra, band, pair_lists, pair_counts):
    freq_ids = jnp.arange(F, dtype=jnp.int32)
    whitened = whiten(spectra, band, freq_ids)
    table = phase_table(freq_ids, jnp.arange(LAGS, dtype=jnp.int32), LAGS, F)
    table_flat = table.reshape(2 * F, LAGS).astype(jnp.float32)
    weight = 1.0 + 3.0 * jnp.arange(LAGS, dtype=jnp.int32).astype(jnp.float32) / LAGS
    blocked = whitened.reshape(BLOCKS, STA_DEV, 3, 2, F)
    offsets = jnp.arange(STEPS, dtype=jnp.int32)
    slot_ids = jnp.arange(P_MAX, dtype=jnp.int32)

    def per_block(block, grad):
        block = block.astype(jnp.int32)
        pairs = pair_lists[block]
        counts = pair_counts[block]
        others = (block - offsets) % BLOCKS
        first = pairs[:, :, 0]
        second = pairs[:, :, 1]
        rows_a = blocked[block][first].astype(jnp.float32)
        rows_b = blocked[others[:, None], second].astype(jnp.float32)
        real_a, imag_a = (rows_a[:, :, :, 0], rows_a[:, :, :, 1])
        real_b, imag_b = (rows_b[:, :, :, 0], rows_b[:, :, :, 1])
        valid = (slot_ids[None, :] < counts[:, None]).astype(jnp.float32)[:, :, None]
        cross_real = lax.optimization_barrier(jnp.sum(real_a * real_b + imag_a * imag_b, axis=2)) * valid
        cross_imag = lax.optimization_barrier(jnp.sum(imag_a * real_b - real_a * imag_b, axis=2)) * valid
        cross = jnp.stack([cross_real, cross_imag], 2).astype(jnp.bfloat16)
        cross_flat = cross.reshape(STEPS * P_MAX, 2 * F).astype(jnp.float32)
        lagged = jnp.dot(cross_flat, table_flat, precision=lax.Precision.HIGHEST)
        energy = lax.optimization_barrier(jnp.sum(weight[None, :] * lagged * lagged, axis=1)) / LAGS
        adjoint = (weight[None, :] * lagged / jnp.sqrt(energy + 1e-05)[:, None]).astype(jnp.bfloat16)
        spectral = jnp.dot(adjoint.astype(jnp.float32), table_flat.T, precision=lax.Precision.HIGHEST)
        spectral = spectral.reshape(STEPS, P_MAX, 2, F)
        adj_real = spectral[:, :, None, 0]
        adj_imag = spectral[:, :, None, 1]
        near = jnp.stack([adj_real * real_b - adj_imag * imag_b, adj_real * imag_b + adj_imag * real_b], 3).astype(jnp.bfloat16)
        far = jnp.stack([adj_real * real_a + adj_imag * imag_a, adj_real * imag_a - adj_imag * real_a], 3).astype(jnp.bfloat16)
        grad = grad.at[block * STA_DEV + first].add(near.astype(jnp.float32))
        grad = grad.at[others[:, None] * STA_DEV + second].add(far.astype(jnp.float32))
        return grad
    grad = lax.fori_loop(0, BLOCKS, per_block, jnp.zeros((STATIONS, 3, 2, F), jnp.float32))
    return grad / jnp.sqrt(jnp.float32(P_MAX))
```

```python
import math

import jax
import jax.numpy as jnp
import numpy as np
from jax import lax
from jax.experimental import pallas as pl
from jax.experimental.pallas import tpu as pltpu
from jax.sharding import Mesh
from jax.sharding import PartitionSpec as P

BF = jnp.bfloat16
F32 = jnp.float32
PLANE = ("yh", "c", "yl", "x")
QUAD = ("yh", "c")
COLS = 8
HALO = (0, 1, 2, -2)
PLACES = {0: (0, 0), 1: (1, 0), 2: (2, 0), 3: (1, 3), 4: (2, 3), 5: (3, 1), 6: (3, 0), 7: (0, 1)}
STEPS = 17
SLOTS = 96
KROWS = 24
NONE = 1024.0


def operator_parts(freq_total):
    lags = 2 * freq_total
    order = np.array(
        [(s % 8) * (freq_total // 8) + (s // 8) * (freq_total // 32) + f for s in range(32) for f in range(freq_total // 32)]
    )
    k = np.arange(-freq_total, 2 * freq_total)
    with np.errstate(divide="ignore"):
        sines = np.where(k == 0, 0.0, -1.5 / np.tan(np.pi * np.where(k == 0, 1, k) / lags))
    f = order[:, None]
    h = order[None, :]
    couple = -(sines[h + f + freq_total] + sines[h - f + freq_total]) / lags
    top = lags + 1.5 * (lags - 1)
    real = np.where(order == 0, 2 * top + 3.0, top - 1.5 + 3.0) / lags
    imag = np.where(order == 0, 0.0, top + 1.5) / lags
    return couple, real, imag, -3.0 / lags


def block_table():
    table = np.zeros((COLS, STEPS, 4, 2), np.int32)
    holder = np.zeros((2, KROWS, 128), np.float32)
    for z in range(COLS):
        for k in range(STEPS):
            for q in range(4):
                yh, c = q // 2, q % 2
                gap = -((c - k) // 2) % COLS
                i, j = PLACES[gap]
                other = (16 * yh + 2 * ((z + HALO[i]) % COLS) + c - k) % 32
                assert (z + HALO[j]) % COLS == other % 16 // 2
                table[z, k, q, 0] = i * 4 + q
                table[z, k, q, 1] = j * 4 + other // 16 * 2 + other % 2
                holder[c, k, :] = i
    return table.reshape(-1), holder


def one_hot(row):
    rows = lax.broadcasted_iota(jnp.int32, (256, 128), 0)
    return (rows == row).astype(F32).astype(BF)


def gather(held, first, second, pick):
    both = jnp.concatenate([held[first], held[second]], axis=1)
    return jnp.dot(both, pick, preferred_element_type=F32)


def cross_body(z_ref, tab_ref, holder_ref, g0, g1, g2, g3, out_ref, idx_ref, held):
    lane = lax.broadcasted_iota(jnp.int32, (KROWS, 128), 1)
    for i, g in enumerate((g0, g1, g2, g3)):
        held[4 * i : 4 * i + 4] = g[:, 0:192, :]
    for side in range(2):
        rolled = []
        for q in range(4):
            where = holder_ref[q % 2]
            lo = 192 + KROWS * side
            rows = jnp.zeros((KROWS, 128), F32)
            for i, g in enumerate((g0, g1, g2, g3)):
                rows = jnp.where(where == float(i), g[q, lo : lo + KROWS, :].astype(F32), rows)
            rows = rows.astype(jnp.int32)
            rolled.append(rows if q == 0 else pltpu.roll(rows, 128 - 32 * q, 1))
        for a in range(3):
            idx_ref[side, a] = jnp.where(lane < 96 - 32 * a, rolled[a], rolled[a + 1] + 128)
    base = z_ref[0] * (STEPS * 8)

    def step(k, carry):
        for a in range(3):
            tile = 3 * k + a
            at = base + k * 8 + a * 2
            u = gather(held, tab_ref[at], tab_ref[at + 2], one_hot(idx_ref[0, a, pl.ds(k, 1), :]))
            v = gather(held, tab_ref[at + 1], tab_ref[at + 3], one_hot(idx_ref[1, a, pl.ds(k, 1), :]))
            real = jnp.zeros((32, 128), F32)
            imag = jnp.zeros((32, 128), F32)
            for c in range(3):
                ur, ui = u[64 * c : 64 * c + 32], u[64 * c + 32 : 64 * c + 64]
                vr, vi = v[64 * c : 64 * c + 32], v[64 * c + 32 : 64 * c + 64]
                real += ur * vr + ui * vi
                imag += ui * vr - ur * vi
            part = jnp.concatenate([real, imag], 0).astype(BF)
            out_ref[tile // 2, :, pl.ds(pl.multiple_of(tile % 2 * 128, 128), 128)] = part
        return carry

    lax.fori_loop(0, STEPS, step, 0)
    for tile in range(3 * STEPS, 64):
        out_ref[tile // 2, :, tile % 2 * 128 : tile % 2 * 128 + 128] = jnp.zeros((64, 128), BF)


def spectral_body(cross_ref, couple_ref, couple_t_ref, diag_ref, out_ref):
    cross = cross_ref[...]
    lags = 2.0 * couple_ref.shape[0]
    size = couple_ref.shape[0]
    c0 = cross[:, 0:32, :].reshape(size, 256)
    c1 = cross[:, 32:64, :].reshape(size, 256)
    f0 = c0.astype(F32)
    f1 = c1.astype(F32)
    y0 = jnp.dot(couple_ref[...], c1, preferred_element_type=F32)
    y0 += diag_ref[:, 0:1] * f0 + (-3.0 / lags) * jnp.sum(f0, axis=0, keepdims=True)
    y1 = jnp.dot(couple_t_ref[...], c0, preferred_element_type=F32) + diag_ref[:, 1:2] * f1
    energy = jnp.sum(y0 * f0 + y1 * f1, axis=0, keepdims=True) / lags
    scale = 1.0 / jnp.sqrt(energy + 1e-5)
    out_ref[:, 0:32, :] = (y0 * scale).astype(BF).reshape(32, 32, 256)
    out_ref[:, 32:64, :] = (y1 * scale).astype(BF).reshape(32, 32, 256)


def sums_body(z_ref, tab_ref, idx_ref, g0, g1, g2, g3, spec_ref, o0, o1, o2, o3, held, acc):
    for i, g in enumerate((g0, g1, g2, g3)):
        held[4 * i : 4 * i + 4] = g[:, 0:192, :]
    acc[...] = jnp.zeros(acc.shape, F32)
    base = z_ref[0] * (STEPS * 8)
    dims = (((1,), (1,)), ((), ()))

    def step(k, carry):
        for a in range(3):
            tile = 3 * k + a
            at = base + k * 8 + a * 2
            ua, va, ub, vb = (tab_ref[at + n] for n in range(4))
            pick_u = one_hot(idx_ref[0, a, pl.ds(k, 1), :])
            pick_v = one_hot(idx_ref[1, a, pl.ds(k, 1), :])
            u = gather(held, ua, ub, pick_u)
            v = gather(held, va, vb, pick_v)
            spec = spec_ref[tile // 2, :, pl.ds(pl.multiple_of(tile % 2 * 128, 128), 128)].astype(F32)
            a0 = spec[0:32]
            a1 = spec[32:64]
            near = []
            far = []
            for c in range(3):
                ur, ui = u[64 * c : 64 * c + 32], u[64 * c + 32 : 64 * c + 64]
                vr, vi = v[64 * c : 64 * c + 32], v[64 * c + 32 : 64 * c + 64]
                near += [a0 * vr - a1 * vi, a0 * vi + a1 * vr]
                far += [a0 * ur + a1 * ui, a0 * ui - a1 * ur]
            near = jnp.concatenate(near, 0).astype(BF)
            far = jnp.concatenate(far, 0).astype(BF)
            to_u = lax.dot_general(near, pick_u, dims, preferred_element_type=F32)
            to_v = lax.dot_general(far, pick_v, dims, preferred_element_type=F32)
            acc[ua] += to_u[:, 0:128]
            acc[ub] += to_u[:, 128:256]
            acc[va] += to_v[:, 0:128]
            acc[vb] += to_v[:, 128:256]
        return carry

    lax.fori_loop(0, STEPS, step, 0)
    o0[...] = acc[0:4]
    for i, o in enumerate((o1, o2, o3)):
        o[...] = acc[4 * i + 4 : 4 * i + 8].astype(BF)


def whiten(spectra, band, first_freq):
    values = spectra.astype(F32).transpose(1, 2, 3, 0)
    meansq = jnp.mean(values * values, axis=(0, 1))
    freq = (first_freq + jnp.arange(values.shape[2], dtype=jnp.int32))[:, None]
    inside = (freq >= band[None, :, 0]) & (freq < band[None, :, 1])
    factor = jnp.where(inside, 1.0 / jnp.sqrt(jnp.maximum(meansq, 0.25)), 0.0)
    return (values * factor).astype(BF)


def on_device(spectra, band, pair_lists, pair_counts):
    stations, comps, parts, bins = spectra.shape
    freq_total = bins * 8
    params = pltpu.CompilerParams(vmem_limit_bytes=56 << 20)
    vmem = pl.BlockSpec(memory_space=pltpu.VMEM)
    smem = pl.BlockSpec(memory_space=pltpu.SMEM)
    zi = lax.axis_index("z").astype(jnp.int32).reshape(1)
    lane = lax.axis_index(("yl", "x"))
    table, holder = block_table()
    table = jnp.asarray(table)

    white = whiten(spectra, band, lane * bins)
    white = white.reshape(comps * parts, 4, bins // 4, stations).transpose(1, 0, 2, 3)
    white = white.reshape(4, comps * parts * bins // 4, stations)
    used = jnp.arange(SLOTS, dtype=jnp.int32)[None, None, :] < pair_counts[0][:, None, None]
    lists = jnp.where(used, pair_lists[0].transpose(0, 2, 1), int(NONE)).astype(BF)
    lists = jnp.pad(lists, ((0, KROWS - STEPS), (0, 0), (0, 128 - SLOTS)), constant_values=NONE)
    lists = lists.transpose(1, 0, 2).reshape(1, 2 * KROWS, 128)
    block = jnp.concatenate([white, jnp.broadcast_to(lists, (4, 2 * KROWS, 128))], 1)
    own = lax.all_to_all(block, QUAD, 0, 0, tiled=True)
    groups = [own]
    for d in HALO[1:]:
        groups.append(lax.ppermute(own, "z", [((z + d) % COLS, z) for z in range(COLS)]))

    cross, index = pl.pallas_call(
        cross_body,
        in_specs=[smem, smem] + [vmem] * 5,
        out_specs=[vmem, vmem],
        out_shape=[
            jax.ShapeDtypeStruct((32, 64, 256), BF),
            jax.ShapeDtypeStruct((2, 3, KROWS, 128), jnp.int32),
        ],
        scratch_shapes=[pltpu.VMEM((16, 192, 128), BF)],
        compiler_params=params,
        name="cross",
    )(zi, table, jnp.asarray(holder), *groups)
    cross = lax.all_to_all(cross, PLANE, 0, 0, tiled=True)

    couple, real, imag, _ = operator_parts(freq_total)
    spectral = pl.pallas_call(
        spectral_body,
        in_specs=[vmem] * 4,
        out_specs=vmem,
        out_shape=jax.ShapeDtypeStruct((32, 64, 256), BF),
        compiler_params=params,
        name="spectral",
    )(
        cross,
        jnp.asarray(couple.astype(np.float32)).astype(BF),
        jnp.asarray(couple.T.astype(np.float32)).astype(BF),
        jnp.asarray(np.stack([real, imag], 1).astype(np.float32)),
    )
    spectral = lax.all_to_all(spectral, PLANE, 0, 0, tiled=True)

    sums = pl.pallas_call(
        sums_body,
        in_specs=[smem, smem] + [vmem] * 6,
        out_specs=[vmem] * 4,
        out_shape=[jax.ShapeDtypeStruct((4, 192, 128), F32)] + [jax.ShapeDtypeStruct((4, 192, 128), BF)] * 3,
        scratch_shapes=[pltpu.VMEM((16, 192, 128), BF), pltpu.VMEM((16, 192, 128), F32)],
        compiler_params=params,
        name="sums",
    )(zi, table, index, *groups, spectral)
    total = sums[0]
    for d, part in zip(HALO[1:], sums[1:]):
        back = lax.ppermute(part, "z", [(z, (z + d) % COLS) for z in range(COLS)])
        total = total + back.astype(F32)
    total = lax.all_to_all(total.astype(BF), QUAD, 0, 0, tiled=True)
    total = total.reshape(4, comps, parts, bins // 4, stations).transpose(4, 1, 2, 0, 3)
    return total.reshape(stations, comps, parts, bins).astype(F32) / math.sqrt(SLOTS)


def solution(mesh):
    fine = Mesh(mesh.devices.reshape(2, 8, 2, 2, 4), ("yh", "z", "c", "yl", "x"))
    blk = ("yh", "z", "c")
    lag = ("yl", "x")
    in_specs = (P(blk, None, None, lag), P(blk, None), P(blk, None, None, None), P(blk, None))
    return jax.shard_map(
        on_device, mesh=fine, in_specs=in_specs, out_specs=P(blk, None, None, lag), check_vma=False
    )
```

```python
import math

import jax
import jax.numpy as jnp
import numpy as np
from jax import lax
from jax.experimental import pallas as pl
from jax.experimental.pallas import tpu as pltpu
from jax.sharding import Mesh
from jax.sharding import PartitionSpec as P

BF = jnp.bfloat16
F32 = jnp.float32
CHIPS = 16
CHIP = ("yh", "z")
ROW = ("c", "yl", "x")
PEERS = 16
HALO = (0, 1, 2, 8, 13)
PLACES = ((0, 0), (1, 0), (2, 0), (0, 4), (1, 4), (2, 4), (3, 2), (3, 1), (3, 0))
STEPS = 17
SLOTS = 96
KROWS = 24
NONE = 1024
WIDE = 4 * SLOTS
TILES = 3 * len(PLACES)
ROWS = 384


def operator_parts(freq_total):
    lags = 2 * freq_total
    share = freq_total // PEERS
    order = np.array([(s % 8) * 2 * share + (s // 8) * share + f for s in range(PEERS) for f in range(share)])
    k = np.arange(-freq_total, 2 * freq_total)
    sines = np.where(k == 0, 0.0, -1.5 / np.tan(np.pi * np.where(k == 0, 1, k) / lags))
    f = order[:, None]
    h = order[None, :]
    couple = -(sines[h + f + freq_total] + sines[h - f + freq_total]) / lags
    top = lags + 1.5 * (lags - 1)
    real = np.where(order == 0, 2 * top + 3.0, top - 1.5 + 3.0) / lags
    imag = np.where(order == 0, 0.0, top + 1.5) / lags
    return couple, real, imag


def lists_of(gap):
    return ((0, 2 * gap - 1), (0, 2 * gap), (1, 2 * gap), (1, 2 * gap + 1))


def one_hot(index_ref, gap, side):
    rows = lax.broadcasted_iota(jnp.int32, (256, 128), 0)
    at = (gap * 2 + side) * 3
    picks = [(rows == index_ref[at + a : at + a + 1, :]).astype(F32).astype(BF) for a in range(3)]
    return jnp.concatenate(picks, 1)


def chip_rows(group):
    return jnp.concatenate([group[0, 0:ROWS, :], group[1, 0:ROWS, :]], 1)


def planes(x):
    return [(x[128 * c : 128 * c + 64], x[128 * c + 64 : 128 * c + 128]) for c in range(3)]


def cross_body(g0, g1, g2, g3, g4, out_ref, index_ref, lists):
    groups = (g0, g1, g2, g3, g4)
    lane = lax.broadcasted_iota(jnp.int32, (1, 128), 1)
    for i, g in enumerate(groups):
        for c in range(2):
            lists[i, c] = g[c, ROWS : ROWS + 2 * KROWS, :].astype(F32).astype(jnp.int32)
    for gap, (i, j) in enumerate(PLACES):
        for side, offsets in enumerate(((0, 0, 128, 128), (128, 0, 128, 0))):
            rolled = []
            for q, (c, k) in enumerate(lists_of(gap)):
                if 0 <= k < STEPS:
                    row = lists[i, c, KROWS * side + k : KROWS * side + k + 1, :] + offsets[q]
                    rolled.append(row if q == 0 else pltpu.roll(row, 128 - 32 * q, 1))
                else:
                    rolled.append(jnp.full((1, 128), NONE, jnp.int32))
            for a in range(3):
                at = (gap * 2 + side) * 3 + a
                index_ref[at : at + 1, :] = jnp.where(lane < 96 - 32 * a, rolled[a], rolled[a + 1])
    for gap, (i, j) in enumerate(PLACES):
        u = jnp.dot(chip_rows(groups[i]), one_hot(index_ref, gap, 0), preferred_element_type=F32)
        v = jnp.dot(chip_rows(groups[j]), one_hot(index_ref, gap, 1), preferred_element_type=F32)
        real = jnp.zeros((64, WIDE), F32)
        imag = jnp.zeros((64, WIDE), F32)
        for (ur, ui), (vr, vi) in zip(planes(u), planes(v)):
            real += ur * vr + ui * vi
            imag += ui * vr - ur * vi
        part = jnp.concatenate([real, imag], 0).astype(BF)
        for a in range(3):
            tile = 3 * gap + a
            half = tile % 2 * 128
            out_ref[tile // 2, :, half : half + 128] = part[:, 128 * a : 128 * a + 128]
    for tile in range(TILES, 2 * PEERS):
        half = tile % 2 * 128
        out_ref[tile // 2, :, half : half + 128] = jnp.zeros((128, 128), BF)


def spectral_body(cross_ref, couple_ref, couple_t_ref, diag_ref, out_ref):
    cross = cross_ref[...]
    size = couple_ref.shape[0]
    lags = 2.0 * size
    c0 = cross[:, 0:64, :].reshape(size, 256)
    c1 = cross[:, 64:128, :].reshape(size, 256)
    f0 = c0.astype(F32)
    f1 = c1.astype(F32)
    y0 = jnp.dot(couple_ref[...], c1, preferred_element_type=F32)
    y0 += diag_ref[:, 0:1] * f0 + (-3.0 / lags) * jnp.sum(f0, axis=0, keepdims=True)
    y1 = jnp.dot(couple_t_ref[...], c0, preferred_element_type=F32) + diag_ref[:, 1:2] * f1
    energy = jnp.sum(y0 * f0 + y1 * f1, axis=0, keepdims=True) / lags
    scale = 1.0 / jnp.sqrt(energy + 1e-5)
    out_ref[:, 0:64, :] = (y0 * scale).astype(BF).reshape(PEERS, 64, 256)
    out_ref[:, 64:128, :] = (y1 * scale).astype(BF).reshape(PEERS, 64, 256)


ORDER = (3, 4, 5, 6, 7, 8, 2, 1, 0)


def sums_body(index_ref, g0, g1, g2, g3, g4, spec_ref, o0, o1, o2, o3, o4, acc):
    groups = (g0, g1, g2, g3, g4)
    dims = (((1,), (1,)), ((), ()))
    begun = set()

    def add(place, value):
        acc[place] = acc[place] + value if place in begun else value
        begun.add(place)

    for gap in ORDER:
        i, j = PLACES[gap]
        pick_u = one_hot(index_ref, gap, 0)
        pick_v = one_hot(index_ref, gap, 1)
        u = jnp.dot(chip_rows(groups[i]), pick_u, preferred_element_type=F32)
        v = jnp.dot(chip_rows(groups[j]), pick_v, preferred_element_type=F32)
        tiles = [3 * gap + a for a in range(3)]
        spec = [spec_ref[t // 2, :, t % 2 * 128 : t % 2 * 128 + 128].astype(F32) for t in tiles]
        spec = jnp.concatenate(spec, 1)
        a0 = spec[0:64]
        a1 = spec[64:128]
        near = []
        far = []
        for (ur, ui), (vr, vi) in zip(planes(u), planes(v)):
            near += [(a0 * vr - a1 * vi).astype(BF), (a0 * vi + a1 * vr).astype(BF)]
            far += [(a0 * ur + a1 * ui).astype(BF), (a0 * ui - a1 * ur).astype(BF)]
        near = jnp.concatenate(near, 0)
        far = jnp.concatenate(far, 0)
        add(i, lax.dot_general(near, pick_u, dims, preferred_element_type=F32))
        add(j, lax.dot_general(far, pick_v, dims, preferred_element_type=F32))
    for i, o in enumerate((o0, o1, o2, o3, o4)):
        for c in range(2):
            o[c] = acc[i, :, 128 * c : 128 * c + 128].astype(o.dtype)


def whiten(spectra, band, first_freq):
    values = spectra.astype(F32).transpose(1, 2, 3, 0)
    meansq = jnp.mean(values * values, axis=(0, 1))
    freq = (first_freq + jnp.arange(values.shape[2], dtype=jnp.int32))[:, None]
    inside = (freq >= band[None, :, 0]) & (freq < band[None, :, 1])
    factor = jnp.where(inside, 1.0 / jnp.sqrt(jnp.maximum(meansq, 0.25)), 0.0)
    return (values * factor).astype(BF)


def on_device(spectra, band, pair_lists, pair_counts):
    stations, comps, parts, bins = spectra.shape
    freq_total = bins * 8
    params = pltpu.CompilerParams(vmem_limit_bytes=24 << 20)
    vmem = pl.BlockSpec(memory_space=pltpu.VMEM)
    lane = lax.axis_index(("yl", "x"))

    white = whiten(spectra, band, lane * bins)
    white = white.reshape(comps * parts, 2, bins // 2, stations).transpose(1, 0, 2, 3)
    white = white.reshape(2, ROWS, stations)
    used = jnp.arange(SLOTS, dtype=jnp.int32)[None, None, :] < pair_counts[0][:, None, None]
    lists = jnp.where(used, pair_lists[0].transpose(0, 2, 1), NONE).astype(BF)
    lists = jnp.pad(lists, ((0, KROWS - STEPS), (0, 0), (0, 128 - SLOTS)), constant_values=NONE)
    lists = lists.transpose(1, 0, 2).reshape(1, 2 * KROWS, 128)
    block = jnp.concatenate([white, jnp.broadcast_to(lists, (2, 2 * KROWS, 128))], 1)
    own = lax.all_to_all(block, "c", 0, 0, tiled=True)
    groups = [own]
    for d in HALO[1:]:
        groups.append(lax.ppermute(own, CHIP, [((w + d) % CHIPS, w) for w in range(CHIPS)]))

    pairs = jax.ShapeDtypeStruct((PEERS, 128, 256), BF)
    cross, index = pl.pallas_call(
        cross_body,
        in_specs=[vmem] * 5,
        out_specs=[vmem, vmem],
        out_shape=[pairs, jax.ShapeDtypeStruct((56, 128), jnp.int32)],
        scratch_shapes=[pltpu.VMEM((5, 2, 2 * KROWS, 128), jnp.int32)],
        compiler_params=params,
        name="cross",
    )(*groups)
    cross = lax.all_to_all(cross, ROW, 0, 0, tiled=True)

    couple, real, imag = operator_parts(freq_total)
    spectral = pl.pallas_call(
        spectral_body,
        in_specs=[vmem] * 4,
        out_specs=vmem,
        out_shape=pairs,
        compiler_params=params,
        name="spectral",
    )(
        cross,
        jnp.asarray(couple.astype(np.float32)).astype(BF),
        jnp.asarray(couple.T.astype(np.float32)).astype(BF),
        jnp.asarray(np.stack([real, imag], 1).astype(np.float32)),
    )
    spectral = lax.all_to_all(spectral, ROW, 0, 0, tiled=True)

    sums = pl.pallas_call(
        sums_body,
        in_specs=[vmem] * 7,
        out_specs=[vmem] * 5,
        out_shape=[jax.ShapeDtypeStruct((2, ROWS, 128), F32)] + [jax.ShapeDtypeStruct((2, ROWS, 128), BF)] * 4,
        scratch_shapes=[pltpu.VMEM((5, ROWS, 256), F32)],
        compiler_params=params,
        name="sums",
    )(index, *groups, spectral)
    total = sums[0]
    for d, part in zip(HALO[1:], sums[1:]):
        back = lax.ppermute(part, CHIP, [(w, (w + d) % CHIPS) for w in range(CHIPS)])
        total = total + back.astype(F32)
    total = lax.all_to_all(total.astype(BF), "c", 0, 0, tiled=True)
    total = total.reshape(2, comps, parts, bins // 2, stations).transpose(4, 1, 2, 0, 3)
    return total.reshape(stations, comps, parts, bins).astype(F32) / math.sqrt(SLOTS)


def solution(mesh):
    fine = Mesh(mesh.devices.reshape(2, 8, 2, 2, 4), ("yh", "z", "c", "yl", "x"))
    blk = ("yh", "z", "c")
    lag = ("yl", "x")
    in_specs = (P(blk, None, None, lag), P(blk, None), P(blk, None, None, None), P(blk, None))
    return jax.shard_map(
        on_device, mesh=fine, in_specs=in_specs, out_specs=P(blk, None, None, lag), check_vma=False
    )
```

```python
import math

import jax
import jax.numpy as jnp
import numpy as np
from jax import lax
from jax.experimental import pallas as pl
from jax.experimental.pallas import tpu as pltpu
from jax.sharding import Mesh
from jax.sharding import PartitionSpec as P

BF = jnp.bfloat16
F32 = jnp.float32
CHIPS = 16
CHIP = ("yh", "z")
ROW = ("c", "yl", "x")
PEERS = 16
HALO = (0, 1, 2, 8, 13)
PLACES = ((0, 0), (1, 0), (2, 0), (0, 4), (1, 4), (2, 4), (3, 2), (3, 1), (3, 0))
STEPS = 17
SLOTS = 96
FRONT = 16
TAIL = 32
NONE = 1024
WIDE = 4 * SLOTS
EARLY = (0, 1, 3, 4)
LATE = (2, 5, 6, 7, 8)
ALONE = tuple((gap, a) for gap in (2, 3, 4, 5, 6) for a in range(3)) + ((1, 0),)
SHARED = ((1, 1), (1, 2), (7, 0), (7, 1), (7, 2), (0, 0), (0, 1), (8, 0))
RESTS = {(8, 1): range(0, 8), (0, 2): range(8, 10), (8, 2): range(10, 12)}
LIST_ROWS = {6: 0, 7: 4, 8: 8, 1: 400, 4: 404, 2: 408, 5: 412, 0: 416, 3: 420}
SENT = {1: (16, 416), 2: (16, 416), 3: (0, 400), 4: (16, 416)}
CHUNK = 128 + 64 + 16
ROWS = 384


def operator_parts(freq_total):
    lags = 2 * freq_total
    share = freq_total // PEERS
    order = np.array([(s % 8) * 2 * share + (s // 8) * share + f for s in range(PEERS) for f in range(share)])
    k = np.arange(-freq_total, 2 * freq_total)
    sines = np.where(k == 0, 0.0, -1.5 / np.tan(np.pi * np.where(k == 0, 1, k) / lags))
    f = order[:, None]
    h = order[None, :]
    couple = -(sines[h + f + freq_total] + sines[h - f + freq_total]) / lags
    top = lags + 1.5 * (lags - 1)
    real = np.where(order == 0, 2 * top + 3.0, top - 1.5 + 3.0) / lags
    imag = np.where(order == 0, 0.0, top + 1.5) / lags
    return couple, real, imag


def lists_of(gap):
    four = ((0, 2 * gap - 1), (0, 2 * gap), (1, 2 * gap), (1, 2 * gap + 1))
    return sorted(four, key=lambda ck: not 0 <= ck[1] < STEPS)


def lanes(shape):
    return lax.broadcasted_iota(jnp.int32, shape, len(shape) - 1)


def turn(x, shift):
    shift %= 128
    return x if shift == 0 else pltpu.roll(x, shift, x.ndim - 1)


def fill_index(index_ref, groups, gaps):
    lane = lanes((1, 128))
    for n, gap in enumerate(gaps):
        row = LIST_ROWS[gap]
        lists = [groups[PLACES[gap][0]](c, row, row + 4).astype(F32).astype(jnp.int32) for c in range(2)]
        for side in range(2):
            rolled = []
            for q, (c, k) in enumerate(lists_of(gap)):
                block = c if side == 0 else (c - k) % 2
                at = 2 * (k - c - 2 * gap + 1) + side
                rolled.append(turn(lists[c][at : at + 1] + 128 * block, -32 * q))
            for a in range(3):
                at = (n * 2 + side) * 3 + a
                index_ref[at : at + 1, :] = jnp.where(lane < 96 - 32 * a, rolled[a], rolled[a + 1])


def one_hot(index_ref, n, side):
    rows = lax.broadcasted_iota(jnp.int32, (256, 128), 0)
    at = (n * 2 + side) * 3
    picks = [(rows == index_ref[at + a : at + a + 1, :]).astype(F32).astype(BF) for a in range(3)]
    return jnp.concatenate(picks, 1)


def both(group):
    return jnp.concatenate([group(0, FRONT, FRONT + ROWS), group(1, FRONT, FRONT + ROWS)], 1)


def by_block(ref, place):
    first = SENT[place][0] if place else 0
    return lambda block, lo, hi: ref[block, lo - first : hi - first, :]


def planes(x):
    return [(x[128 * c : 128 * c + 64], x[128 * c + 64 : 128 * c + 128]) for c in range(3)]


def cross_of(groups, index_ref, rows_ref, n, gap):
    i, j = PLACES[gap]
    u = jnp.dot(both(groups[i]), one_hot(index_ref, n, 0), preferred_element_type=F32)
    v = jnp.dot(both(groups[j]), one_hot(index_ref, n, 1), preferred_element_type=F32)
    rows_ref[n, 0] = u.astype(BF)
    rows_ref[n, 1] = v.astype(BF)
    real = jnp.zeros((64, WIDE), F32)
    imag = jnp.zeros((64, WIDE), F32)
    for (ur, ui), (vr, vi) in zip(planes(u), planes(v)):
        real += ur * vr + ui * vi
        imag += ui * vr - ur * vi
    return real, imag


def put_pairs(out_ref, gap, all_real, all_imag):
    lane = lanes((64, 128))
    slot = lanes((16, 128)) // 16
    for a in range(3):
        real = all_real[:, 128 * a : 128 * a + 128]
        imag = all_imag[:, 128 * a : 128 * a + 128]
        if (gap, a) in ALONE:
            peer = ALONE.index((gap, a))
            out_ref[peer, 0:64, :] = real.astype(BF)
            out_ref[peer, 64:128, :] = imag.astype(BF)
        elif (gap, a) in SHARED:
            peer = 2 * SHARED.index((gap, a))
            out_ref[peer, 128:192, :] = jnp.where(lane < 64, real, turn(imag, 64)).astype(BF)
            out_ref[peer + 1, 128:192, :] = jnp.where(lane < 64, turn(real, 64), imag).astype(BF)
        else:
            for m, peer in enumerate(RESTS[gap, a]):
                rest = jnp.zeros((16, 128), F32)
                for s in range(4):
                    rows = slice(16 * s, 16 * s + 16)
                    rest = jnp.where(slot == s, turn(real[rows], 16 * (s - m)), rest)
                    rest = jnp.where(slot == s + 4, turn(imag[rows], 16 * (s + 4 - m)), rest)
                out_ref[peer, 192:208, :] = rest.astype(BF)


def early_cross_body(g0, g1, g4, out_ref, index_ref, rows_ref):
    groups = {0: by_block(g0, 0), 1: by_block(g1, 1), 4: by_block(g4, 4)}
    fill_index(index_ref, groups, EARLY)
    for n, gap in enumerate(EARLY):
        put_pairs(out_ref, gap, *cross_of(groups, index_ref, rows_ref, n, gap))
    for peer in range(12, PEERS):
        out_ref[peer, 192:208, :] = jnp.zeros((16, 128), BF)


def late_cross_body(g0, g1, g2, g3, g4, begun, out_ref, index_ref, rows_ref):
    groups = [by_block(g, place) for place, g in enumerate((g0, g1, g2, g3, g4))]
    fill_index(index_ref, groups, LATE)
    for n, gap in enumerate(LATE):
        put_pairs(out_ref, gap, *cross_of(groups, index_ref, rows_ref, n, gap))


def spectral_body(cross_ref, couple_ref, couple_t_ref, diag_ref, out_ref):
    size = couple_ref.shape[0]
    lags = 2.0 * size
    lane = lanes((PEERS, 64, 128))
    slot = lanes((PEERS, 16, 128)) // 16
    half = cross_ref[:, 128:192, :].astype(F32)
    rest = cross_ref[:, 192:208, :].astype(F32)
    real_rest = jnp.concatenate([turn(rest, 64 - 16 * s) for s in range(4)], 1)
    imag_rest = jnp.concatenate([turn(rest, -16 * s) for s in range(4)], 1)
    real_half = jnp.where(lane < 64, half, real_rest).astype(BF)
    imag_half = jnp.where(lane < 64, turn(half, 64), imag_rest).astype(BF)
    c0 = jnp.concatenate([cross_ref[:, 0:64, :], real_half], 2).reshape(size, 256)
    c1 = jnp.concatenate([cross_ref[:, 64:128, :], imag_half], 2).reshape(size, 256)
    f0 = c0.astype(F32)
    f1 = c1.astype(F32)
    y0 = jnp.dot(couple_ref[...], c1, preferred_element_type=F32)
    y0 += diag_ref[:, 0:1] * f0 + (-3.0 / lags) * jnp.sum(f0, axis=0, keepdims=True)
    y1 = jnp.dot(couple_t_ref[...], c0, preferred_element_type=F32) + diag_ref[:, 1:2] * f1
    energy = jnp.sum(y0 * f0 + y1 * f1, axis=0, keepdims=True) / lags
    scale = 1.0 / jnp.sqrt(energy + 1e-5)
    a0 = (y0 * scale).reshape(PEERS, 64, 256)
    a1 = (y1 * scale).reshape(PEERS, 64, 256)
    out_ref[:, 0:64, :] = a0[:, :, 0:128].astype(BF)
    out_ref[:, 64:128, :] = a1[:, :, 0:128].astype(BF)
    a0 = a0[:, :, 128:256]
    a1 = a1[:, :, 128:256]
    out_ref[:, 128:192, :] = jnp.where(lane < 64, a0, turn(a1, 64)).astype(BF)
    rest = jnp.zeros((PEERS, 16, 128), F32)
    for s in range(4):
        rows = slice(16 * s, 16 * s + 16)
        rest = jnp.where(slot == s, turn(a0[:, rows], 16 * s - 64), rest)
        rest = jnp.where(slot == s + 4, turn(a1[:, rows], 16 * s), rest)
    out_ref[:, 192:208, :] = rest.astype(BF)


def spectra_of(spec_ref, gap, a):
    lane = lanes((64, 128))
    slot = lanes((16, 128)) // 16
    if (gap, a) in ALONE:
        peer = ALONE.index((gap, a))
        return spec_ref[peer, 0:64, :].astype(F32), spec_ref[peer, 64:128, :].astype(F32)
    if (gap, a) in SHARED:
        peer = 2 * SHARED.index((gap, a))
        left = spec_ref[peer, 128:192, :].astype(F32)
        right = spec_ref[peer + 1, 128:192, :].astype(F32)
        return jnp.where(lane < 64, left, turn(right, 64)), jnp.where(lane < 64, turn(left, 64), right)
    real = [jnp.zeros((16, 128), F32)] * 4
    imag = [jnp.zeros((16, 128), F32)] * 4
    for m, peer in enumerate(RESTS[gap, a]):
        rest = spec_ref[peer, 192:208, :].astype(F32)
        for s in range(4):
            real[s] = jnp.where(slot == m, turn(rest, 16 * (m - s)), real[s])
            imag[s] = jnp.where(slot == m, turn(rest, 16 * (m - s - 4)), imag[s])
    return jnp.concatenate(real, 0), jnp.concatenate(imag, 0)


def sums_of(rows_ref, index_ref, spec_ref, n, gap):
    i, j = PLACES[gap]
    dims = (((1,), (1,)), ((), ()))
    pick_u = one_hot(index_ref, n, 0)
    pick_v = one_hot(index_ref, n, 1)
    u = rows_ref[n, 0].astype(F32)
    v = rows_ref[n, 1].astype(F32)
    tiles = [spectra_of(spec_ref, gap, a) for a in range(3)]
    a0 = jnp.concatenate([t[0] for t in tiles], 1)
    a1 = jnp.concatenate([t[1] for t in tiles], 1)
    near = []
    far = []
    for (ur, ui), (vr, vi) in zip(planes(u), planes(v)):
        near += [(a0 * vr - a1 * vi).astype(BF), (a0 * vi + a1 * vr).astype(BF)]
        far += [(a0 * ur + a1 * ui).astype(BF), (a0 * ui - a1 * ur).astype(BF)]
    near = lax.dot_general(jnp.concatenate(near, 0), pick_u, dims, preferred_element_type=F32)
    far = lax.dot_general(jnp.concatenate(far, 0), pick_v, dims, preferred_element_type=F32)
    return (i, near), (j, far)


def sums_body(early_ref, early_rows, late_ref, late_rows, spec_ref, o0, o1, o2, o3, o4, acc):
    begun = set()
    for index_ref, rows_ref, gaps in ((late_ref, late_rows, LATE), (early_ref, early_rows, EARLY)):
        for n, gap in enumerate(gaps):
            for place, value in sums_of(rows_ref, index_ref, spec_ref, n, gap):
                acc[place] = acc[place] + value if place in begun else value
                begun.add(place)
    for place, o in enumerate((o0, o1, o2, o3, o4)):
        for c in range(2):
            o[c] = acc[place, :, 128 * c : 128 * c + 128].astype(o.dtype)


def block_body(at_ref, spectra_ref, tables_ref, out_ref):
    core, first_freq = at_ref[0], at_ref[1]
    band = tables_ref[STEPS]
    counts = tables_ref[STEPS + 1, 0:1, :]
    values = [[spectra_ref[c, r].astype(F32) for r in range(2)] for c in range(3)]
    power = jnp.zeros(values[0][0].shape, F32)
    for pair in values:
        power += pair[0] * pair[0] + pair[1] * pair[1]
    freq = first_freq + lax.broadcasted_iota(jnp.int32, power.shape, 0)
    inside = (freq >= band[0:1]) & (freq < band[1:2])
    factor = jnp.where(inside, 1.0 / jnp.sqrt(jnp.maximum(power / 6.0, 0.25)), 0.0)
    for c in range(3):
        for r in range(2):
            white = (values[c][r] * factor).astype(BF)
            row = FRONT + 128 * c + 64 * r
            for h in range(2):
                out_ref[h, row : row + 64, :] = white[64 * h : 64 * h + 64]
    lane = lanes((2, 128))
    unused = jnp.full((4, 128), NONE, jnp.int32)
    rows = {}
    for gap, row in LIST_ROWS.items():
        both_offsets = []
        for n in range(2):
            k = 2 * gap - 1 + n + core
            at = jnp.clip(k, 0, STEPS - 1)
            count = jnp.sum(jnp.where(lanes((1, 128)) == k, counts, 0), axis=1, keepdims=True)
            both_offsets.append(jnp.where(lane < count, tables_ref[at], NONE))
        rows[row] = jnp.concatenate(both_offsets, 0)
    front = jnp.concatenate([rows.get(4 * n, unused) for n in range(4)], 0)
    tail = jnp.concatenate([rows.get(FRONT + ROWS + 4 * n, unused) for n in range(8)], 0)
    for h in range(2):
        out_ref[h, 0:FRONT, :] = front.astype(F32).astype(BF)
        out_ref[h, FRONT + ROWS :, :] = tail.astype(F32).astype(BF)


def on_device(spectra, band, pair_lists, pair_counts):
    stations, comps, parts, bins = spectra.shape
    freq_total = bins * 8
    params = pltpu.CompilerParams(vmem_limit_bytes=24 << 20)
    vmem = pl.BlockSpec(memory_space=pltpu.VMEM)
    lane = lax.axis_index(("yl", "x"))

    def by_chip(x, shift):
        return lax.ppermute(x, CHIP, [((w + shift) % CHIPS, w) for w in range(CHIPS)])

    core = lax.axis_index("c")
    smem = pl.BlockSpec(memory_space=pltpu.SMEM)
    tables = jnp.concatenate(
        [
            jnp.pad(pair_lists[0].transpose(0, 2, 1), ((0, 0), (0, 0), (0, 128 - SLOTS))),
            band.T[None],
            jnp.pad(pair_counts[None], ((0, 0), (0, 1), (0, 128 - STEPS))),
        ],
        0,
    )
    block = pl.pallas_call(
        block_body,
        in_specs=[smem, vmem, vmem],
        out_specs=vmem,
        out_shape=jax.ShapeDtypeStruct((2, FRONT + ROWS + TAIL, stations), BF),
        compiler_params=params,
        name="block",
    )(
        jnp.stack([core, lane * bins]).astype(jnp.int32),
        spectra.transpose(1, 2, 3, 0),
        tables,
    )
    own = lax.all_to_all(block, "c", 0, 0, tiled=True)
    groups = [own]
    for place, (lo, hi) in SENT.items():
        groups.append(by_chip(own[:, lo:hi], HALO[place]))

    pairs = jax.ShapeDtypeStruct((PEERS, CHUNK, 128), BF)
    kept = [jax.ShapeDtypeStruct((n, 2, ROWS, WIDE), BF) for n in (len(EARLY), len(LATE))]
    cross, early, early_rows = pl.pallas_call(
        early_cross_body,
        in_specs=[vmem] * 3,
        out_specs=[vmem] * 3,
        out_shape=[pairs, jax.ShapeDtypeStruct((24, 128), jnp.int32), kept[0]],
        compiler_params=params,
        cost_estimate=pl.CostEstimate(flops=600000000, transcendentals=0, bytes_accessed=6291456),
        name="early_cross",
    )(groups[0], groups[1], groups[4])
    cross, late, late_rows = pl.pallas_call(
        late_cross_body,
        in_specs=[vmem] * 6,
        out_specs=[vmem] * 3,
        out_shape=[pairs, jax.ShapeDtypeStruct((32, 128), jnp.int32), kept[1]],
        input_output_aliases={5: 0},
        compiler_params=params,
        cost_estimate=pl.CostEstimate(flops=800000000, transcendentals=0, bytes_accessed=6291456),
        name="late_cross",
    )(*groups, cross)
    cross = lax.all_to_all(cross, ROW, 0, 0, tiled=True)

    couple, real, imag = operator_parts(freq_total)
    spectral = pl.pallas_call(
        spectral_body,
        in_specs=[vmem] * 4,
        out_specs=vmem,
        out_shape=pairs,
        compiler_params=params,
        cost_estimate=pl.CostEstimate(flops=1100000000, transcendentals=0, bytes_accessed=6291456),
        name="spectral",
    )(
        cross,
        jnp.asarray(couple.astype(np.float32)).astype(BF),
        jnp.asarray(couple.T.astype(np.float32)).astype(BF),
        jnp.asarray(np.stack([real, imag], 1).astype(np.float32)),
    )
    spectral = lax.all_to_all(spectral, ROW, 0, 0, tiled=True)

    chip = jax.ShapeDtypeStruct((2, ROWS, 128), BF)
    sums = pl.pallas_call(
        sums_body,
        in_specs=[vmem] * 5,
        out_specs=[vmem] * 5,
        out_shape=[jax.ShapeDtypeStruct((2, ROWS, 128), F32)] + [chip] * 4,
        scratch_shapes=[pltpu.VMEM((5, ROWS, 256), F32)],
        compiler_params=params,
        name="sums",
    )(early, early_rows, late, late_rows, spectral)
    total = sums[0]
    for place in (4, 1, 2, 3):
        total = total + by_chip(sums[place], -HALO[place]).astype(F32)
    total = lax.all_to_all(total.astype(BF), "c", 0, 0, tiled=True)
    total = total.reshape(2, comps, parts, bins // 2, stations).transpose(4, 1, 2, 0, 3)
    return total.reshape(stations, comps, parts, bins).astype(F32) / math.sqrt(SLOTS)


def solution(mesh):
    fine = Mesh(mesh.devices.reshape(2, 8, 2, 2, 4), ("yh", "z", "c", "yl", "x"))
    blk = ("yh", "z", "c")
    lag = ("yl", "x")
    in_specs = (P(blk, None, None, lag), P(blk, None), P(blk, None, None, None), P(blk, None))
    return jax.shard_map(
        on_device, mesh=fine, in_specs=in_specs, out_specs=P(blk, None, None, lag), check_vma=False
    )
```

```python
import math

import jax
import jax.numpy as jnp
import numpy as np
from jax import lax
from jax.experimental import pallas as pl
from jax.experimental.pallas import tpu as pltpu
from jax.sharding import Mesh
from jax.sharding import PartitionSpec as P

BF = jnp.bfloat16
F32 = jnp.float32
CHIPS = 16
CHIP = ("yh", "z")
ROW = ("c", "yl", "x")
PEERS = 16
HALO = (0, 1, 2, 8, 13)
PLACES = ((0, 0), (1, 0), (2, 0), (0, 4), (1, 4), (2, 4), (3, 2), (3, 1), (3, 0))
STEPS = 17
SLOTS = 96
FRONT = 16
TAIL = 32
NONE = 1024
WIDE = 4 * SLOTS
EARLY = (0, 1, 3, 4)
LATE = (2, 5, 6, 7, 8)
ALONE = tuple((gap, a) for gap in (2, 3, 4, 5, 6) for a in range(3)) + ((1, 0),)
SHARED = ((1, 1), (1, 2), (7, 0), (7, 1), (7, 2), (0, 0), (0, 1), (8, 0))
RESTS = {(8, 1): range(0, 8), (0, 2): range(8, 10), (8, 2): range(10, 12)}
LIST_ROWS = {6: 0, 7: 4, 8: 8, 1: 400, 4: 404, 2: 408, 5: 412, 0: 416, 3: 420}
SENT = {1: (16, 416), 2: (16, 416), 3: (0, 400), 4: (16, 416)}
CHUNK = 128 + 64 + 16
ROWS = 384


def operator_parts(freq_total):
    lags = 2 * freq_total
    share = freq_total // PEERS
    order = np.array([(s % 8) * 2 * share + (s // 8) * share + f for s in range(PEERS) for f in range(share)])
    k = np.arange(-freq_total, 2 * freq_total)
    sines = np.where(k == 0, 0.0, -1.5 / np.tan(np.pi * np.where(k == 0, 1, k) / lags))
    f = order[:, None]
    h = order[None, :]
    couple = -(sines[h + f + freq_total] + sines[h - f + freq_total]) / lags
    top = lags + 1.5 * (lags - 1)
    real = np.where(order == 0, 2 * top + 3.0, top - 1.5 + 3.0) / lags
    imag = np.where(order == 0, 0.0, top + 1.5) / lags
    return couple, real, imag


def lists_of(gap):
    four = ((0, 2 * gap - 1), (0, 2 * gap), (1, 2 * gap), (1, 2 * gap + 1))
    return sorted(four, key=lambda ck: not 0 <= ck[1] < STEPS)


def lanes(shape):
    return lax.broadcasted_iota(jnp.int32, shape, len(shape) - 1)


def turn(x, shift):
    shift %= 128
    return x if shift == 0 else pltpu.roll(x, shift, x.ndim - 1)


def fill_index(index_ref, groups, gaps):
    lane = lanes((1, 128))
    for n, gap in enumerate(gaps):
        row = LIST_ROWS[gap]
        lists = [groups[PLACES[gap][0]](c, row, row + 4).astype(F32).astype(jnp.int32) for c in range(2)]
        for side in range(2):
            rolled = []
            for q, (c, k) in enumerate(lists_of(gap)):
                block = c if side == 0 else (c - k) % 2
                at = 2 * (k - c - 2 * gap + 1) + side
                rolled.append(turn(lists[c][at : at + 1] + 128 * block, -32 * q))
            for a in range(3):
                at = (n * 2 + side) * 3 + a
                index_ref[at : at + 1, :] = jnp.where(lane < 96 - 32 * a, rolled[a], rolled[a + 1])


def one_hot(index_ref, n, side):
    rows = lax.broadcasted_iota(jnp.int32, (256, 128), 0)
    at = (n * 2 + side) * 3
    picks = [(rows == index_ref[at + a : at + a + 1, :]).astype(F32).astype(BF) for a in range(3)]
    return jnp.concatenate(picks, 1)


def both(group):
    return jnp.concatenate([group(0, FRONT, FRONT + ROWS), group(1, FRONT, FRONT + ROWS)], 1)


def by_block(ref, place):
    first = SENT[place][0] if place else 0
    return lambda block, lo, hi: ref[block, lo - first : hi - first, :]


def planes(x):
    return [(x[128 * c : 128 * c + 64], x[128 * c + 64 : 128 * c + 128]) for c in range(3)]


def cross_of(groups, index_ref, rows_ref, n, gap):
    i, j = PLACES[gap]
    u = jnp.dot(both(groups[i]), one_hot(index_ref, n, 0), preferred_element_type=F32)
    v = jnp.dot(both(groups[j]), one_hot(index_ref, n, 1), preferred_element_type=F32)
    rows_ref[n, 0] = u.astype(BF)
    rows_ref[n, 1] = v.astype(BF)
    real = jnp.zeros((64, WIDE), F32)
    imag = jnp.zeros((64, WIDE), F32)
    for (ur, ui), (vr, vi) in zip(planes(u), planes(v)):
        real += ur * vr + ui * vi
        imag += ui * vr - ur * vi
    return real, imag


def put_pairs(out_ref, gap, all_real, all_imag):
    lane = lanes((64, 128))
    slot = lanes((16, 128)) // 16
    for a in range(3):
        real = all_real[:, 128 * a : 128 * a + 128]
        imag = all_imag[:, 128 * a : 128 * a + 128]
        if (gap, a) in ALONE:
            peer = ALONE.index((gap, a))
            out_ref[peer, 0:64, :] = real.astype(BF)
            out_ref[peer, 64:128, :] = imag.astype(BF)
        elif (gap, a) in SHARED:
            peer = 2 * SHARED.index((gap, a))
            out_ref[peer, 128:192, :] = jnp.where(lane < 64, real, turn(imag, 64)).astype(BF)
            out_ref[peer + 1, 128:192, :] = jnp.where(lane < 64, turn(real, 64), imag).astype(BF)
        else:
            for m, peer in enumerate(RESTS[gap, a]):
                rest = jnp.zeros((16, 128), F32)
                for s in range(4):
                    rows = slice(16 * s, 16 * s + 16)
                    rest = jnp.where(slot == s, turn(real[rows], 16 * (s - m)), rest)
                    rest = jnp.where(slot == s + 4, turn(imag[rows], 16 * (s + 4 - m)), rest)
                out_ref[peer, 192:208, :] = rest.astype(BF)


def early_cross_body(g0, g1, g4, out_ref, index_ref, rows_ref):
    groups = {0: by_block(g0, 0), 1: by_block(g1, 1), 4: by_block(g4, 4)}
    fill_index(index_ref, groups, EARLY)
    for n, gap in enumerate(EARLY):
        put_pairs(out_ref, gap, *cross_of(groups, index_ref, rows_ref, n, gap))
    for peer in range(12, PEERS):
        out_ref[peer, 192:208, :] = jnp.zeros((16, 128), BF)


def late_cross_body(g0, g1, g2, g3, g4, begun, out_ref, index_ref, rows_ref):
    groups = [by_block(g, place) for place, g in enumerate((g0, g1, g2, g3, g4))]
    fill_index(index_ref, groups, LATE)
    for n, gap in enumerate(LATE):
        put_pairs(out_ref, gap, *cross_of(groups, index_ref, rows_ref, n, gap))


def spectral_body(cross_ref, couple_ref, couple_t_ref, diag_ref, out_ref):
    size = couple_ref.shape[0]
    lags = 2.0 * size
    lane = lanes((PEERS, 64, 128))
    slot = lanes((PEERS, 16, 128)) // 16
    half = cross_ref[:, 128:192, :].astype(F32)
    rest = cross_ref[:, 192:208, :].astype(F32)
    real_rest = jnp.concatenate([turn(rest, 64 - 16 * s) for s in range(4)], 1)
    imag_rest = jnp.concatenate([turn(rest, -16 * s) for s in range(4)], 1)
    real_half = jnp.where(lane < 64, half, real_rest).astype(BF)
    imag_half = jnp.where(lane < 64, turn(half, 64), imag_rest).astype(BF)
    c0 = jnp.concatenate([cross_ref[:, 0:64, :], real_half], 2).reshape(size, 256)
    c1 = jnp.concatenate([cross_ref[:, 64:128, :], imag_half], 2).reshape(size, 256)
    f0 = c0.astype(F32)
    f1 = c1.astype(F32)
    y0 = jnp.dot(couple_ref[...], c1, preferred_element_type=F32)
    y0 += diag_ref[:, 0:1] * f0 + (-3.0 / lags) * jnp.sum(f0, axis=0, keepdims=True)
    y1 = jnp.dot(couple_t_ref[...], c0, preferred_element_type=F32) + diag_ref[:, 1:2] * f1
    energy = jnp.sum(y0 * f0 + y1 * f1, axis=0, keepdims=True) / lags
    scale = 1.0 / jnp.sqrt(energy + 1e-5)
    a0 = (y0 * scale).reshape(PEERS, 64, 256)
    a1 = (y1 * scale).reshape(PEERS, 64, 256)
    out_ref[:, 0:64, :] = a0[:, :, 0:128].astype(BF)
    out_ref[:, 64:128, :] = a1[:, :, 0:128].astype(BF)
    a0 = a0[:, :, 128:256]
    a1 = a1[:, :, 128:256]
    out_ref[:, 128:192, :] = jnp.where(lane < 64, a0, turn(a1, 64)).astype(BF)
    rest = jnp.zeros((PEERS, 16, 128), F32)
    for s in range(4):
        rows = slice(16 * s, 16 * s + 16)
        rest = jnp.where(slot == s, turn(a0[:, rows], 16 * s - 64), rest)
        rest = jnp.where(slot == s + 4, turn(a1[:, rows], 16 * s), rest)
    out_ref[:, 192:208, :] = rest.astype(BF)


def spectra_of(spec_ref, gap, a):
    lane = lanes((64, 128))
    slot = lanes((16, 128)) // 16
    if (gap, a) in ALONE:
        peer = ALONE.index((gap, a))
        return spec_ref[peer, 0:64, :].astype(F32), spec_ref[peer, 64:128, :].astype(F32)
    if (gap, a) in SHARED:
        peer = 2 * SHARED.index((gap, a))
        left = spec_ref[peer, 128:192, :].astype(F32)
        right = spec_ref[peer + 1, 128:192, :].astype(F32)
        return jnp.where(lane < 64, left, turn(right, 64)), jnp.where(lane < 64, turn(left, 64), right)
    real = [jnp.zeros((16, 128), F32)] * 4
    imag = [jnp.zeros((16, 128), F32)] * 4
    for m, peer in enumerate(RESTS[gap, a]):
        rest = spec_ref[peer, 192:208, :].astype(F32)
        for s in range(4):
            real[s] = jnp.where(slot == m, turn(rest, 16 * (m - s)), real[s])
            imag[s] = jnp.where(slot == m, turn(rest, 16 * (m - s - 4)), imag[s])
    return jnp.concatenate(real, 0), jnp.concatenate(imag, 0)


def sums_of(rows_ref, index_ref, spec_ref, n, gap):
    i, j = PLACES[gap]
    dims = (((1,), (1,)), ((), ()))
    pick_u = one_hot(index_ref, n, 0)
    pick_v = one_hot(index_ref, n, 1)
    u = rows_ref[n, 0].astype(F32)
    v = rows_ref[n, 1].astype(F32)
    tiles = [spectra_of(spec_ref, gap, a) for a in range(3)]
    a0 = jnp.concatenate([t[0] for t in tiles], 1)
    a1 = jnp.concatenate([t[1] for t in tiles], 1)
    near = []
    far = []
    for (ur, ui), (vr, vi) in zip(planes(u), planes(v)):
        near += [(a0 * vr - a1 * vi).astype(BF), (a0 * vi + a1 * vr).astype(BF)]
        far += [(a0 * ur + a1 * ui).astype(BF), (a0 * ui - a1 * ur).astype(BF)]
    near = lax.dot_general(jnp.concatenate(near, 0), pick_u, dims, preferred_element_type=F32)
    far = lax.dot_general(jnp.concatenate(far, 0), pick_v, dims, preferred_element_type=F32)
    return (i, near), (j, far)


def sums_body(early_ref, early_rows, late_ref, late_rows, spec_ref, o0, o1, o2, o3, o4, acc):
    begun = set()
    for index_ref, rows_ref, gaps in ((late_ref, late_rows, LATE), (early_ref, early_rows, EARLY)):
        for n, gap in enumerate(gaps):
            for place, value in sums_of(rows_ref, index_ref, spec_ref, n, gap):
                acc[place] = acc[place] + value if place in begun else value
                begun.add(place)
    for place, o in enumerate((o0, o1, o2, o3, o4)):
        for c in range(2):
            o[c] = acc[place, :, 128 * c : 128 * c + 128].astype(o.dtype)


def block_body(at_ref, spectra_ref, tables_ref, out_ref):
    core, first_freq = at_ref[0], at_ref[1]
    band = tables_ref[STEPS]
    counts = tables_ref[STEPS + 1, 0:1, :]
    values = [[spectra_ref[c, r].astype(F32) for r in range(2)] for c in range(3)]
    power = jnp.zeros(values[0][0].shape, F32)
    for pair in values:
        power += pair[0] * pair[0] + pair[1] * pair[1]
    freq = first_freq + lax.broadcasted_iota(jnp.int32, power.shape, 0)
    inside = (freq >= band[0:1]) & (freq < band[1:2])
    factor = jnp.where(inside, 1.0 / jnp.sqrt(jnp.maximum(power / 6.0, 0.25)), 0.0)
    for c in range(3):
        for r in range(2):
            white = (values[c][r] * factor).astype(BF)
            row = FRONT + 128 * c + 64 * r
            for h in range(2):
                out_ref[h, row : row + 64, :] = white[64 * h : 64 * h + 64]
    lane = lanes((2, 128))
    unused = jnp.full((4, 128), NONE, jnp.int32)
    rows = {}
    for gap, row in LIST_ROWS.items():
        both_offsets = []
        for n in range(2):
            k = 2 * gap - 1 + n + core
            at = jnp.clip(k, 0, STEPS - 1)
            count = jnp.sum(jnp.where(lanes((1, 128)) == k, counts, 0), axis=1, keepdims=True)
            both_offsets.append(jnp.where(lane < count, tables_ref[at], NONE))
        rows[row] = jnp.concatenate(both_offsets, 0)
    front = jnp.concatenate([rows.get(4 * n, unused) for n in range(4)], 0)
    tail = jnp.concatenate([rows.get(FRONT + ROWS + 4 * n, unused) for n in range(8)], 0)
    for h in range(2):
        out_ref[h, 0:FRONT, :] = front.astype(F32).astype(BF)
        out_ref[h, FRONT + ROWS :, :] = tail.astype(F32).astype(BF)


def on_device(spectra, band, pair_lists, pair_counts):
    stations, comps, parts, bins = spectra.shape
    freq_total = bins * 8
    params = pltpu.CompilerParams(vmem_limit_bytes=24 << 20)
    vmem = pl.BlockSpec(memory_space=pltpu.VMEM)
    lane = lax.axis_index(("yl", "x"))

    def by_chip(x, shift):
        return lax.ppermute(x, CHIP, [((w + shift) % CHIPS, w) for w in range(CHIPS)])

    core = lax.axis_index("c")
    smem = pl.BlockSpec(memory_space=pltpu.SMEM)
    tables = jnp.concatenate(
        [
            jnp.pad(pair_lists[0].transpose(0, 2, 1), ((0, 0), (0, 0), (0, 128 - SLOTS))),
            band.T[None],
            jnp.pad(pair_counts[None], ((0, 0), (0, 1), (0, 128 - STEPS))),
        ],
        0,
    )
    block = pl.pallas_call(
        block_body,
        in_specs=[smem, vmem, vmem],
        out_specs=vmem,
        out_shape=jax.ShapeDtypeStruct((2, FRONT + ROWS + TAIL, stations), BF),
        compiler_params=params,
        name="block",
    )(
        jnp.stack([core, lane * bins]).astype(jnp.int32),
        spectra.transpose(1, 2, 3, 0),
        tables,
    )
    own = lax.all_to_all(block, "c", 0, 0, tiled=True)
    groups = [own]
    for place, (lo, hi) in SENT.items():
        groups.append(by_chip(own[:, lo:hi], HALO[place]))

    pairs = jax.ShapeDtypeStruct((PEERS, CHUNK, 128), BF)
    kept = [jax.ShapeDtypeStruct((n, 2, ROWS, WIDE), BF) for n in (len(EARLY), len(LATE))]
    cross, early, early_rows = pl.pallas_call(
        early_cross_body,
        in_specs=[vmem] * 3,
        out_specs=[vmem] * 3,
        out_shape=[pairs, jax.ShapeDtypeStruct((24, 128), jnp.int32), kept[0]],
        compiler_params=params,
        cost_estimate=pl.CostEstimate(flops=600000000, transcendentals=0, bytes_accessed=6291456),
        name="early_cross",
    )(groups[0], groups[1], groups[4])
    cross, late, late_rows = pl.pallas_call(
        late_cross_body,
        in_specs=[vmem] * 6,
        out_specs=[vmem] * 3,
        out_shape=[pairs, jax.ShapeDtypeStruct((32, 128), jnp.int32), kept[1]],
        input_output_aliases={5: 0},
        compiler_params=params,
        cost_estimate=pl.CostEstimate(flops=800000000, transcendentals=0, bytes_accessed=6291456),
        name="late_cross",
    )(*groups, cross)
    cross = lax.all_to_all(cross, ROW, 0, 0, tiled=True)

    couple, real, imag = operator_parts(freq_total)
    spectral = pl.pallas_call(
        spectral_body,
        in_specs=[vmem] * 4,
        out_specs=vmem,
        out_shape=pairs,
        compiler_params=params,
        cost_estimate=pl.CostEstimate(flops=1100000000, transcendentals=0, bytes_accessed=6291456),
        name="spectral",
    )(
        cross,
        jnp.asarray(couple.astype(np.float32)).astype(BF),
        jnp.asarray(couple.T.astype(np.float32)).astype(BF),
        jnp.asarray(np.stack([real, imag], 1).astype(np.float32)),
    )
    spectral = lax.all_to_all(spectral, ROW, 0, 0, tiled=True)

    chip = jax.ShapeDtypeStruct((2, ROWS, 128), BF)
    sums = pl.pallas_call(
        sums_body,
        in_specs=[vmem] * 5,
        out_specs=[vmem] * 5,
        out_shape=[jax.ShapeDtypeStruct((2, ROWS, 128), F32)] + [chip] * 4,
        scratch_shapes=[pltpu.VMEM((5, ROWS, 256), F32)],
        compiler_params=params,
        name="sums",
    )(early, early_rows, late, late_rows, spectral)
    total = sums[0]
    for place in (1, 2, 4, 3):
        total = total + by_chip(sums[place], -HALO[place]).astype(F32)
    total = lax.all_to_all(total.astype(BF), "c", 0, 0, tiled=True)
    total = total.reshape(2, comps, parts, bins // 2, stations).transpose(4, 1, 2, 0, 3)
    return total.reshape(stations, comps, parts, bins).astype(F32) / math.sqrt(SLOTS)


def solution(mesh):
    fine = Mesh(mesh.devices.reshape(2, 8, 2, 2, 4), ("yh", "z", "c", "yl", "x"))
    blk = ("yh", "z", "c")
    lag = ("yl", "x")
    in_specs = (P(blk, None, None, lag), P(blk, None), P(blk, None, None, None), P(blk, None))
    return jax.shard_map(
        on_device, mesh=fine, in_specs=in_specs, out_specs=P(blk, None, None, lag), check_vma=False
    )
```

```python
import math

import jax
import jax.numpy as jnp
import numpy as np
from jax import lax
from jax.experimental import pallas as pl
from jax.experimental.pallas import tpu as pltpu
from jax.sharding import Mesh
from jax.sharding import PartitionSpec as P

BF = jnp.bfloat16
F32 = jnp.float32
CHIPS = 16
CHIP = ("yh", "z")
ROW = ("c", "yl", "x")
PEERS = 16
HALO = (0, 1, 2, 8, 13)
PLACES = ((0, 0), (1, 0), (2, 0), (0, 4), (1, 4), (2, 4), (3, 2), (3, 1), (3, 0))
STEPS = 17
SLOTS = 96
FRONT = 16
TAIL = 32
NONE = 1024
WIDE = 4 * SLOTS
EARLY = (0, 2, 3, 5)
LATE = (1, 4, 6, 7, 8)
ALONE = tuple((gap, a) for gap in (2, 3, 4, 5, 6) for a in range(3)) + ((1, 0),)
SHARED = ((1, 1), (1, 2), (7, 0), (7, 1), (7, 2), (0, 0), (0, 1), (8, 0))
RESTS = {(8, 1): range(0, 8), (0, 2): range(8, 10), (8, 2): range(10, 12)}
LIST_ROWS = {6: 0, 7: 4, 8: 8, 1: 400, 4: 404, 2: 408, 5: 412, 0: 416, 3: 420}
SENT = {1: (16, 416), 2: (16, 416), 3: (0, 400), 4: (16, 416)}
CHUNK = 128 + 64 + 16
ROWS = 384


def operator_parts(freq_total):
    lags = 2 * freq_total
    share = freq_total // PEERS
    order = np.array([(s % 8) * 2 * share + (s // 8) * share + f for s in range(PEERS) for f in range(share)])
    k = np.arange(-freq_total, 2 * freq_total)
    sines = np.where(k == 0, 0.0, -1.5 / np.tan(np.pi * np.where(k == 0, 1, k) / lags))
    f = order[:, None]
    h = order[None, :]
    couple = -(sines[h + f + freq_total] + sines[h - f + freq_total]) / lags
    top = lags + 1.5 * (lags - 1)
    real = np.where(order == 0, 2 * top + 3.0, top - 1.5 + 3.0) / lags
    imag = np.where(order == 0, 0.0, top + 1.5) / lags
    return couple, real, imag


def lists_of(gap):
    four = ((0, 2 * gap - 1), (0, 2 * gap), (1, 2 * gap), (1, 2 * gap + 1))
    return sorted(four, key=lambda ck: not 0 <= ck[1] < STEPS)


def lanes(shape):
    return lax.broadcasted_iota(jnp.int32, shape, len(shape) - 1)


def turn(x, shift):
    shift %= 128
    return x if shift == 0 else pltpu.roll(x, shift, x.ndim - 1)


def fill_index(index_ref, groups, gaps):
    lane = lanes((1, 128))
    for n, gap in enumerate(gaps):
        row = LIST_ROWS[gap]
        lists = [groups[PLACES[gap][0]](c, row, row + 4).astype(F32).astype(jnp.int32) for c in range(2)]
        for side in range(2):
            rolled = []
            for q, (c, k) in enumerate(lists_of(gap)):
                block = c if side == 0 else (c - k) % 2
                at = 2 * (k - c - 2 * gap + 1) + side
                rolled.append(turn(lists[c][at : at + 1] + 128 * block, -32 * q))
            for a in range(3):
                at = (n * 2 + side) * 3 + a
                index_ref[at : at + 1, :] = jnp.where(lane < 96 - 32 * a, rolled[a], rolled[a + 1])


def one_hot(index_ref, n, side):
    rows = lax.broadcasted_iota(jnp.int32, (256, 128), 0)
    at = (n * 2 + side) * 3
    picks = [(rows == index_ref[at + a : at + a + 1, :]).astype(F32).astype(BF) for a in range(3)]
    return jnp.concatenate(picks, 1)


def both(group):
    return jnp.concatenate([group(0, FRONT, FRONT + ROWS), group(1, FRONT, FRONT + ROWS)], 1)


def by_block(ref, place):
    first = SENT[place][0] if place else 0
    return lambda block, lo, hi: ref[block, lo - first : hi - first, :]


def planes(x):
    return [(x[128 * c : 128 * c + 64], x[128 * c + 64 : 128 * c + 128]) for c in range(3)]


def cross_of(groups, index_ref, rows_ref, n, gap):
    i, j = PLACES[gap]
    u = jnp.dot(both(groups[i]), one_hot(index_ref, n, 0), preferred_element_type=F32)
    v = jnp.dot(both(groups[j]), one_hot(index_ref, n, 1), preferred_element_type=F32)
    rows_ref[n, 0] = u.astype(BF)
    rows_ref[n, 1] = v.astype(BF)
    real = jnp.zeros((64, WIDE), F32)
    imag = jnp.zeros((64, WIDE), F32)
    for (ur, ui), (vr, vi) in zip(planes(u), planes(v)):
        real += ur * vr + ui * vi
        imag += ui * vr - ur * vi
    return real, imag


def put_pairs(out_ref, gap, all_real, all_imag):
    lane = lanes((64, 128))
    slot = lanes((16, 128)) // 16
    for a in range(3):
        real = all_real[:, 128 * a : 128 * a + 128]
        imag = all_imag[:, 128 * a : 128 * a + 128]
        if (gap, a) in ALONE:
            peer = ALONE.index((gap, a))
            out_ref[peer, 0:64, :] = real.astype(BF)
            out_ref[peer, 64:128, :] = imag.astype(BF)
        elif (gap, a) in SHARED:
            peer = 2 * SHARED.index((gap, a))
            out_ref[peer, 128:192, :] = jnp.where(lane < 64, real, turn(imag, 64)).astype(BF)
            out_ref[peer + 1, 128:192, :] = jnp.where(lane < 64, turn(real, 64), imag).astype(BF)
        else:
            for m, peer in enumerate(RESTS[gap, a]):
                rest = jnp.zeros((16, 128), F32)
                for s in range(4):
                    rows = slice(16 * s, 16 * s + 16)
                    rest = jnp.where(slot == s, turn(real[rows], 16 * (s - m)), rest)
                    rest = jnp.where(slot == s + 4, turn(imag[rows], 16 * (s + 4 - m)), rest)
                out_ref[peer, 192:208, :] = rest.astype(BF)


def early_cross_body(g0, g2, g4, out_ref, index_ref, rows_ref):
    groups = {0: by_block(g0, 0), 2: by_block(g2, 2), 4: by_block(g4, 4)}
    fill_index(index_ref, groups, EARLY)
    for n, gap in enumerate(EARLY):
        put_pairs(out_ref, gap, *cross_of(groups, index_ref, rows_ref, n, gap))
    for peer in range(12, PEERS):
        out_ref[peer, 192:208, :] = jnp.zeros((16, 128), BF)


def late_cross_body(g0, g2, g4, g3, g1, begun, out_ref, index_ref, rows_ref):
    groups = [by_block(g, place) for place, g in enumerate((g0, g1, g2, g3, g4))]
    fill_index(index_ref, groups, LATE)
    for n, gap in enumerate(LATE):
        put_pairs(out_ref, gap, *cross_of(groups, index_ref, rows_ref, n, gap))


def spectral_body(cross_ref, couple_ref, couple_t_ref, diag_ref, out_ref):
    size = couple_ref.shape[0]
    lags = 2.0 * size
    lane = lanes((PEERS, 64, 128))
    slot = lanes((PEERS, 16, 128)) // 16
    half = cross_ref[:, 128:192, :].astype(F32)
    rest = cross_ref[:, 192:208, :].astype(F32)
    real_rest = jnp.concatenate([turn(rest, 64 - 16 * s) for s in range(4)], 1)
    imag_rest = jnp.concatenate([turn(rest, -16 * s) for s in range(4)], 1)
    real_half = jnp.where(lane < 64, half, real_rest).astype(BF)
    imag_half = jnp.where(lane < 64, turn(half, 64), imag_rest).astype(BF)
    c0 = jnp.concatenate([cross_ref[:, 0:64, :], real_half], 2).reshape(size, 256)
    c1 = jnp.concatenate([cross_ref[:, 64:128, :], imag_half], 2).reshape(size, 256)
    f0 = c0.astype(F32)
    f1 = c1.astype(F32)
    y0 = jnp.dot(couple_ref[...], c1, preferred_element_type=F32)
    y0 += diag_ref[:, 0:1] * f0 + (-3.0 / lags) * jnp.sum(f0, axis=0, keepdims=True)
    y1 = jnp.dot(couple_t_ref[...], c0, preferred_element_type=F32) + diag_ref[:, 1:2] * f1
    energy = jnp.sum(y0 * f0 + y1 * f1, axis=0, keepdims=True) / lags
    scale = 1.0 / jnp.sqrt(energy + 1e-5)
    a0 = (y0 * scale).reshape(PEERS, 64, 256)
    a1 = (y1 * scale).reshape(PEERS, 64, 256)
    out_ref[:, 0:64, :] = a0[:, :, 0:128].astype(BF)
    out_ref[:, 64:128, :] = a1[:, :, 0:128].astype(BF)
    a0 = a0[:, :, 128:256]
    a1 = a1[:, :, 128:256]
    out_ref[:, 128:192, :] = jnp.where(lane < 64, a0, turn(a1, 64)).astype(BF)
    rest = jnp.zeros((PEERS, 16, 128), F32)
    for s in range(4):
        rows = slice(16 * s, 16 * s + 16)
        rest = jnp.where(slot == s, turn(a0[:, rows], 16 * s - 64), rest)
        rest = jnp.where(slot == s + 4, turn(a1[:, rows], 16 * s), rest)
    out_ref[:, 192:208, :] = rest.astype(BF)


def spectra_of(spec_ref, gap, a):
    lane = lanes((64, 128))
    slot = lanes((16, 128)) // 16
    if (gap, a) in ALONE:
        peer = ALONE.index((gap, a))
        return spec_ref[peer, 0:64, :].astype(F32), spec_ref[peer, 64:128, :].astype(F32)
    if (gap, a) in SHARED:
        peer = 2 * SHARED.index((gap, a))
        left = spec_ref[peer, 128:192, :].astype(F32)
        right = spec_ref[peer + 1, 128:192, :].astype(F32)
        return jnp.where(lane < 64, left, turn(right, 64)), jnp.where(lane < 64, turn(left, 64), right)
    real = [jnp.zeros((16, 128), F32)] * 4
    imag = [jnp.zeros((16, 128), F32)] * 4
    for m, peer in enumerate(RESTS[gap, a]):
        rest = spec_ref[peer, 192:208, :].astype(F32)
        for s in range(4):
            real[s] = jnp.where(slot == m, turn(rest, 16 * (m - s)), real[s])
            imag[s] = jnp.where(slot == m, turn(rest, 16 * (m - s - 4)), imag[s])
    return jnp.concatenate(real, 0), jnp.concatenate(imag, 0)


def sums_of(rows_ref, index_ref, spec_ref, n, gap):
    i, j = PLACES[gap]
    dims = (((1,), (1,)), ((), ()))
    pick_u = one_hot(index_ref, n, 0)
    pick_v = one_hot(index_ref, n, 1)
    u = rows_ref[n, 0].astype(F32)
    v = rows_ref[n, 1].astype(F32)
    tiles = [spectra_of(spec_ref, gap, a) for a in range(3)]
    a0 = jnp.concatenate([t[0] for t in tiles], 1)
    a1 = jnp.concatenate([t[1] for t in tiles], 1)
    near = []
    far = []
    for (ur, ui), (vr, vi) in zip(planes(u), planes(v)):
        near += [(a0 * vr - a1 * vi).astype(BF), (a0 * vi + a1 * vr).astype(BF)]
        far += [(a0 * ur + a1 * ui).astype(BF), (a0 * ui - a1 * ur).astype(BF)]
    near = lax.dot_general(jnp.concatenate(near, 0), pick_u, dims, preferred_element_type=F32)
    far = lax.dot_general(jnp.concatenate(far, 0), pick_v, dims, preferred_element_type=F32)
    return (i, near), (j, far)


def sums_body(early_ref, early_rows, late_ref, late_rows, spec_ref, o0, o1, o2, o3, o4, acc):
    begun = set()
    for index_ref, rows_ref, gaps in ((late_ref, late_rows, LATE), (early_ref, early_rows, EARLY)):
        for n, gap in enumerate(gaps):
            for place, value in sums_of(rows_ref, index_ref, spec_ref, n, gap):
                acc[place] = acc[place] + value if place in begun else value
                begun.add(place)
    for place, o in enumerate((o0, o1, o2, o3, o4)):
        for c in range(2):
            o[c] = acc[place, :, 128 * c : 128 * c + 128].astype(o.dtype)


def block_body(at_ref, spectra_ref, tables_ref, out_ref):
    core, first_freq = at_ref[0], at_ref[1]
    band = tables_ref[STEPS]
    counts = tables_ref[STEPS + 1, 0:1, :]
    values = [[spectra_ref[c, r].astype(F32) for r in range(2)] for c in range(3)]
    power = jnp.zeros(values[0][0].shape, F32)
    for pair in values:
        power += pair[0] * pair[0] + pair[1] * pair[1]
    freq = first_freq + lax.broadcasted_iota(jnp.int32, power.shape, 0)
    inside = (freq >= band[0:1]) & (freq < band[1:2])
    factor = jnp.where(inside, 1.0 / jnp.sqrt(jnp.maximum(power / 6.0, 0.25)), 0.0)
    for c in range(3):
        for r in range(2):
            white = (values[c][r] * factor).astype(BF)
            row = FRONT + 128 * c + 64 * r
            for h in range(2):
                out_ref[h, row : row + 64, :] = white[64 * h : 64 * h + 64]
    lane = lanes((2, 128))
    unused = jnp.full((4, 128), NONE, jnp.int32)
    rows = {}
    for gap, row in LIST_ROWS.items():
        both_offsets = []
        for n in range(2):
            k = 2 * gap - 1 + n + core
            at = jnp.clip(k, 0, STEPS - 1)
            count = jnp.sum(jnp.where(lanes((1, 128)) == k, counts, 0), axis=1, keepdims=True)
            both_offsets.append(jnp.where(lane < count, tables_ref[at], NONE))
        rows[row] = jnp.concatenate(both_offsets, 0)
    front = jnp.concatenate([rows.get(4 * n, unused) for n in range(4)], 0)
    tail = jnp.concatenate([rows.get(FRONT + ROWS + 4 * n, unused) for n in range(8)], 0)
    for h in range(2):
        out_ref[h, 0:FRONT, :] = front.astype(F32).astype(BF)
        out_ref[h, FRONT + ROWS :, :] = tail.astype(F32).astype(BF)


def on_device(spectra, band, pair_lists, pair_counts):
    stations, comps, parts, bins = spectra.shape
    freq_total = bins * 8
    params = pltpu.CompilerParams(vmem_limit_bytes=24 << 20)
    vmem = pl.BlockSpec(memory_space=pltpu.VMEM)
    lane = lax.axis_index(("yl", "x"))

    def by_chip(x, shift):
        return lax.ppermute(x, CHIP, [((w + shift) % CHIPS, w) for w in range(CHIPS)])

    core = lax.axis_index("c")
    smem = pl.BlockSpec(memory_space=pltpu.SMEM)
    tables = jnp.concatenate(
        [
            jnp.pad(pair_lists[0].transpose(0, 2, 1), ((0, 0), (0, 0), (0, 128 - SLOTS))),
            band.T[None],
            jnp.pad(pair_counts[None], ((0, 0), (0, 1), (0, 128 - STEPS))),
        ],
        0,
    )
    block = pl.pallas_call(
        block_body,
        in_specs=[smem, vmem, vmem],
        out_specs=vmem,
        out_shape=jax.ShapeDtypeStruct((2, FRONT + ROWS + TAIL, stations), BF),
        compiler_params=params,
        name="block",
    )(
        jnp.stack([core, lane * bins]).astype(jnp.int32),
        spectra.transpose(1, 2, 3, 0),
        tables,
    )
    own = lax.all_to_all(block, "c", 0, 0, tiled=True)
    groups = [own]
    for place, (lo, hi) in SENT.items():
        groups.append(by_chip(own[:, lo:hi], HALO[place]))

    pairs = jax.ShapeDtypeStruct((PEERS, CHUNK, 128), BF)
    kept = [jax.ShapeDtypeStruct((n, 2, ROWS, WIDE), BF) for n in (len(EARLY), len(LATE))]
    cross, early, early_rows = pl.pallas_call(
        early_cross_body,
        in_specs=[vmem] * 3,
        out_specs=[vmem] * 3,
        out_shape=[pairs, jax.ShapeDtypeStruct((24, 128), jnp.int32), kept[0]],
        compiler_params=params,
        cost_estimate=pl.CostEstimate(flops=600000000, transcendentals=0, bytes_accessed=6291456),
        name="early_cross",
    )(groups[0], groups[2], groups[4])
    cross, late, late_rows = pl.pallas_call(
        late_cross_body,
        in_specs=[vmem] * 6,
        out_specs=[vmem] * 3,
        out_shape=[pairs, jax.ShapeDtypeStruct((32, 128), jnp.int32), kept[1]],
        input_output_aliases={5: 0},
        compiler_params=params,
        cost_estimate=pl.CostEstimate(flops=800000000, transcendentals=0, bytes_accessed=6291456),
        name="late_cross",
    )(groups[0], groups[2], groups[4], groups[3], groups[1], cross)
    cross = lax.all_to_all(cross, ROW, 0, 0, tiled=True)

    couple, real, imag = operator_parts(freq_total)
    spectral = pl.pallas_call(
        spectral_body,
        in_specs=[vmem] * 4,
        out_specs=vmem,
        out_shape=pairs,
        compiler_params=params,
        cost_estimate=pl.CostEstimate(flops=1100000000, transcendentals=0, bytes_accessed=6291456),
        name="spectral",
    )(
        cross,
        jnp.asarray(couple.astype(np.float32)).astype(BF),
        jnp.asarray(couple.T.astype(np.float32)).astype(BF),
        jnp.asarray(np.stack([real, imag], 1).astype(np.float32)),
    )
    spectral = lax.all_to_all(spectral, ROW, 0, 0, tiled=True)

    chip = jax.ShapeDtypeStruct((2, ROWS, 128), BF)
    sums = pl.pallas_call(
        sums_body,
        in_specs=[vmem] * 5,
        out_specs=[vmem] * 5,
        out_shape=[jax.ShapeDtypeStruct((2, ROWS, 128), F32)] + [chip] * 4,
        scratch_shapes=[pltpu.VMEM((5, ROWS, 256), F32)],
        compiler_params=params,
        name="sums",
    )(early, early_rows, late, late_rows, spectral)
    total = sums[0]
    for place in (1, 2, 4, 3):
        total = total + by_chip(sums[place], -HALO[place]).astype(F32)
    total = lax.all_to_all(total.astype(BF), "c", 0, 0, tiled=True)
    total = total.reshape(2, comps, parts, bins // 2, stations).transpose(4, 1, 2, 0, 3)
    return total.reshape(stations, comps, parts, bins).astype(F32) / math.sqrt(SLOTS)


def solution(mesh):
    fine = Mesh(mesh.devices.reshape(2, 8, 2, 2, 4), ("yh", "z", "c", "yl", "x"))
    blk = ("yh", "z", "c")
    lag = ("yl", "x")
    in_specs = (P(blk, None, None, lag), P(blk, None), P(blk, None, None, None), P(blk, None))
    return jax.shard_map(
        on_device, mesh=fine, in_specs=in_specs, out_specs=P(blk, None, None, lag), check_vma=False
    )
```
